256 devices in a mesh: expert: 8 (over x, core), fsdp: 32 (over z, y).
Axes of the slice: x: 4, y: 4, z: 8, core: 2. Of those that a mesh axis runs over, the one named last changes fastest.
Arguments:
- teacher_tokens: bfloat16 [4096, 7168], P('fsdp'), may hold values from -6 to 6
- routes: int32 [4096, 8], P('fsdp'), may hold values from 0 to 255, as said below
- slots: int32 [4096, 8], P('fsdp'), may hold values from -1 to 3, as said below
- route_weights: float32 [4096, 8], P('fsdp'), may hold values from 0.1 to 1
- gate_proj: bfloat16 [32, 7168, 1024], P('fsdp', None, 'expert'), may hold values from -0.0625 to 0.0625
- up_proj: bfloat16 [32, 7168, 1024], P('fsdp', None, 'expert'), may hold values from -0.0625 to 0.0625
- down_proj: bfloat16 [32, 1024, 7168], P('fsdp', 'expert'), may hold values from -0.1875 to 0.1875
- projector: bfloat16 [7168, 5120], P('fsdp', 'expert'), may hold values from -0.0625 to 0.0625
- student_input: bfloat16 [4096, 5120], P('fsdp'), may hold values from -6 to 6
- student_weight: bfloat16 [5120, 5120], P('fsdp', 'expert'), may hold values from -0.078125 to 0.078125
Outputs:
- target: bfloat16 [4096, 5120], P('fsdp', 'expert')
- grad_weight: float32 [5120, 5120], P('fsdp', 'expert')
The draws below stay inside these ranges and needn't reach their ends.
Inputs may be any that keep to these rules, and one draw needn't show every extreme that they name: `routes`: each row names 8 different experts. In each aligned block of 128 rows every expert below 32 is named by 1 to 4 rows, and some expert below 32, drawn from the seed, is named by exactly 4 rows in every block. `slots`: for a choice naming an expert below 32: its slot, different for the choices of one block that name that expert; -1 for every other choice.
All inputs are finite; a program needn't handle non-finite values.
Results may differ from the reference program's by a relative error of at most 0.02.
Values may be sent and summed in bfloat16 or wider, within the bound.
No kernel may reach another device: no remote copies, remote signals or barrier semaphores. Data moves between devices by JAX's collectives and lax.ppermute only.
A program may use at most 128 MiB of HBM per device.

```python
import math
import jax
import jax.numpy as jnp
from jax import lax

D = 7168
FF = 1024
EXPERTS = 256
TOPK = 8
D_S = 5120
TOK_DEV = 128
TOKENS = 4096
WAVE = 32
CAP = 4
FF_DEV = 128
N_EXPERT = 8


def route_plan(key):
    blocks = TOKENS // TOK_DEV
    half = WAVE // 2
    keys = jax.random.split(jax.random.fold_in(key, 7), 6)
    levels = jax.random.randint(keys[0], (2, half), 1, CAP + 1)
    hottest = jax.random.randint(keys[1], (2, 1), 0, half)
    is_hot = jnp.arange(half)[None, :] == hottest
    levels = jnp.where(is_hot, CAP, levels)
    raw_counts = jax.random.randint(keys[2], (blocks, 2, half), 0, 1 << 20)
    counts = raw_counts % levels[None] + 1
    counts = jnp.where(is_hot[None], CAP, counts)
    perm_keys = jax.random.split(keys[3], blocks * 2)

    def shuffle_deck(single_key):
        return jax.random.permutation(single_key, TOK_DEV)
    orders = jax.vmap(shuffle_deck)(perm_keys).reshape(blocks, 2, TOK_DEV)
    expert_local = orders // CAP
    slot_local = orders % CAP
    clipped = jnp.minimum(expert_local, half - 1)
    limits = jnp.take_along_axis(counts, clipped, axis=2)
    valid = (orders < half * CAP) & (slot_local < limits)
    wave_ids = expert_local + jnp.arange(2)[None, :, None] * half
    valid_rows = valid.transpose(0, 2, 1).reshape(TOKENS, 2)
    wave_rows = wave_ids.transpose(0, 2, 1).reshape(TOKENS, 2)
    slot_rows = slot_local.transpose(0, 2, 1).reshape(TOKENS, 2)
    scores = jax.random.randint(keys[4], (TOKENS, EXPERTS - WAVE), 0, 1 << 20) * EXPERTS + jnp.arange(EXPERTS - WAVE)
    _, others = lax.top_k(scores, TOPK)
    others = others + WAVE
    head_ids = jnp.where(valid_rows, wave_rows, others[:, :2])
    head_slots = jnp.where(valid_rows, slot_rows, -1)
    all_ids = jnp.concatenate([head_ids, others[:, 2:]], axis=1).astype(jnp.int32)
    all_slots = jnp.concatenate([head_slots, jnp.full((TOKENS, TOPK - 2), -1, jnp.int32)], axis=1).astype(jnp.int32)
    column_scores = jax.random.randint(keys[5], (TOKENS, TOPK), 0, 1 << 20) * TOPK + jnp.arange(TOPK)
    column_order = jnp.argsort(column_scores, axis=1)
    return (jnp.take_along_axis(all_ids, column_order, axis=1), jnp.take_along_axis(all_slots, column_order, axis=1))


def draw_routes(key, part):
    return route_plan(key)[0]


def draw_slots(key, part):
    return route_plan(key)[1]


def spiked(result, rng, source, target, parts, factor):
    def block_of(axis_at):
        return (jnp.arange(result.shape[axis_at]) // (result.shape[axis_at] // parts)).reshape((-1,) + (1,) * (result.ndim - 1 - axis_at))

    near = jax.random.permutation(rng, parts)[block_of(target)]
    second = (block_of(target) + parts // 2) % parts
    return jnp.where((block_of(source) == near) | (block_of(source) == second), factor * result, result)


def steps_of(stream_key, shape, shards, least, high):
    factor_of, own = 1.0, jax.random.fold_in(stream_key, 6)
    for position, parts in shards:
        steps = jnp.exp(jax.random.uniform(jax.random.fold_in(own, position), (parts,), jnp.float32, least / len(shards), high / len(shards)))
        factor_of = factor_of * jnp.repeat(steps, shape[position] // parts).reshape([-1 if axis == position else 1 for axis in range(len(shape))])
    return factor_of


def centred(key, extent, width, limit, shards=(), kind=jnp.bfloat16):
    level = steps_of(key, extent, shards, -0.22, 0.18) if shards else 1.0
    array = jax.random.normal(key, extent, jnp.float32) * width * level
    return jnp.minimum(jnp.maximum(array, -limit), limit).astype(kind)


def noise_with(stream_key, shape, scale, reach, shards, heavy, kind=jnp.bfloat16):
    array = scale * jax.random.normal(stream_key, shape, jnp.float32)
    if shards:
        array = array * steps_of(stream_key, shape, shards, -0.22, 0.18)
    return jnp.clip(spiked(array, jax.random.fold_in(stream_key, 3), *heavy), -reach, reach).astype(kind)


def setup_inputs(seed: int = 0) -> dict:
    key_of = jax.random.split(jax.random.key(seed), 11)
    return {
        "teacher_tokens": centred(key_of[0], (TOKENS, D), 1.0, 6.0, ((0, 32),)),
        "routes": draw_routes(jax.random.fold_in(key_of[10], 71), 0),
        "slots": draw_slots(jax.random.fold_in(key_of[10], 71), 0),
        "route_weights": jnp.clip(jnp.exp(math.log(1.0) - 2.3025851 * jax.random.uniform(key_of[3], (TOKENS, TOPK), jnp.float32) ** steps_of(key_of[3], (TOKENS, TOPK), ((0, 32),), -0.2, 0.2)), 0.1, 1.0),
        "gate_proj": centred(key_of[4], (WAVE, D, FF), D ** -0.5, 0.0625, ((0, 32), (2, 8))),
        "up_proj": centred(key_of[5], (WAVE, D, FF), D ** -0.5, 0.0625, ((0, 32), (2, 8))),
        "down_proj": centred(key_of[6], (WAVE, FF, D), FF ** -0.5, 0.1875, ((0, 32), (1, 8))),
        "projector": centred(key_of[7], (D, D_S), D ** -0.5, 0.0625, ((0, 32), (1, 8))),
        "student_input": noise_with(key_of[8], (TOKENS, D_S), 1.0, 6.0, ((0, 32),), (0, 1, 32, 2.75)),
        "student_weight": centred(key_of[9], (D_S, D_S), D_S ** -0.5, 0.078125, ((0, 32), (1, 8))),
    }


def reference(teacher_tokens, routes, slots, route_weights, gate_proj, up_proj, down_proj, projector, student_input, student_weight):
    blocks = TOKENS // TOK_DEV
    slot_ids = jnp.arange(WAVE * CAP, dtype=jnp.int32)
    slot_index = jnp.where(routes < WAVE, routes * CAP + slots, -1).astype(jnp.int32)
    index_blocks = slot_index.reshape(blocks, TOK_DEV, TOPK)
    token_blocks = teacher_tokens.reshape(blocks, TOK_DEV, D)

    def dispatch_block(operands):
        block_index, block_rows = operands
        dispatch_mask = lax.optimization_barrier(jnp.sum((block_index[:, :, None] == slot_ids).astype(jnp.float32), axis=1)).astype(jnp.bfloat16)
        return jnp.dot(dispatch_mask.T, block_rows, preferred_element_type=jnp.float32).astype(jnp.bfloat16)
    dispatched = lax.map(dispatch_block, (index_blocks, token_blocks))
    by_expert = dispatched.reshape(blocks, WAVE, CAP, D).transpose(1, 0, 2, 3).reshape(WAVE, blocks * CAP, D)

    def expert_step(operands):
        row_block, gate_w, up_w, down_w = operands
        gate_act = jnp.dot(row_block, gate_w, preferred_element_type=jnp.float32)
        up_act = jnp.dot(row_block, up_w, preferred_element_type=jnp.float32)
        hidden = (jax.nn.silu(gate_act) * up_act).astype(jnp.bfloat16)
        running = jnp.zeros((row_block.shape[0], D), jnp.float32)
        for group_index in range(N_EXPERT):
            low = group_index * FF_DEV
            group_part = jnp.dot(hidden[:, low:low + FF_DEV], down_w[low:low + FF_DEV], preferred_element_type=jnp.float32).astype(jnp.bfloat16)
            group_part = lax.optimization_barrier(group_part)
            running = running + group_part.astype(jnp.float32)
        return running.astype(jnp.bfloat16)
    expert_out = lax.map(expert_step, (by_expert, gate_proj, up_proj, down_proj))
    returned = expert_out.reshape(WAVE, blocks, CAP, D).transpose(1, 0, 2, 3).reshape(blocks, WAVE * CAP, D)
    weight_blocks = route_weights.reshape(blocks, TOK_DEV, TOPK)

    def combine_block(operands):
        block_index, block_weights, returned_rows = operands
        running = jnp.zeros((TOK_DEV, D), jnp.float32)
        for choice_index in range(TOPK):
            column = block_index[:, choice_index]
            picked = jnp.take(returned_rows, jnp.maximum(column, 0), axis=0).astype(jnp.float32)
            factor = jnp.where(column >= 0, block_weights[:, choice_index], 0.0)
            running = running + factor[:, None] * picked
        return running.astype(jnp.bfloat16)
    teacher_out = lax.map(combine_block, (index_blocks, weight_blocks, returned)).reshape(TOKENS, D)
    projected = jnp.dot(teacher_out, projector, preferred_element_type=jnp.float32)
    student_out = jnp.dot(student_input, student_weight, preferred_element_type=jnp.float32)
    error = ((student_out - projected) * (1.0 / math.sqrt(TOKENS))).astype(jnp.bfloat16)

    def grad_block(running, operands):
        input_rows, error_rows = operands
        block_term = jnp.dot(input_rows.T, error_rows, preferred_element_type=jnp.float32).astype(jnp.bfloat16)
        block_term = lax.optimization_barrier(block_term)
        return (running + block_term.astype(jnp.float32), None)
    gradient, _ = lax.scan(grad_block, jnp.zeros((D_S, D_S), jnp.float32), (student_input.reshape(blocks, TOK_DEV, D_S), error.reshape(blocks, TOK_DEV, D_S)))
    return (projected.astype(jnp.bfloat16), gradient)
```

```python
import math

import jax
import jax.numpy as jnp
from jax import lax
from jax.experimental import pallas as pl
from jax.experimental.pallas import tpu as pltpu
from jax.sharding import Mesh
from jax.sharding import PartitionSpec as P

CAP = 4
BF = jnp.bfloat16
F32 = jnp.float32
VMEM = pl.BlockSpec(memory_space=pltpu.VMEM)
SMEM = pl.BlockSpec(memory_space=pltpu.SMEM)
PARAMS = pltpu.CompilerParams(vmem_limit_bytes=48 * 1024 * 1024)


def shifted(value, axis, hop):
    size = lax.axis_size(axis)
    return lax.ppermute(value, axis, [(i, (i - hop) % size) for i in range(size)])


def gather_expert(value):
    own = [value] + [shifted(value, "x", hop) for hop in (1, 2, 3)]
    other = [shifted(block, "c", 1) for block in own]
    return own + other


def ffn_kernel(order, *refs):
    blocks, (gate, up, down, keep, send) = refs[:8], refs[8:]
    width = blocks[0].shape[1]
    gate_act = jnp.zeros((blocks[0].shape[0], gate.shape[1]), F32)
    up_act = jnp.zeros_like(gate_act)
    for k in range(8):
        rows = pl.ds(pl.multiple_of(order[k] * width, 128), width)
        block = blocks[k][...]
        gate_act += jnp.dot(block, gate[rows, :], preferred_element_type=F32)
        up_act += jnp.dot(block, up[rows, :], preferred_element_type=F32)
    hidden = (gate_act / (1.0 + jnp.exp(-gate_act)) * up_act).astype(BF)
    for k in (4, 5, 6, 7, 0, 1, 2, 3):
        cols = pl.ds(pl.multiple_of(order[k] * width, 128), width)
        part = jnp.dot(hidden, down[:, cols], preferred_element_type=F32).astype(BF)
        if k < 4:
            keep[k] = part
        else:
            send[k - 4] = part


def ffn(order, blocks, gate, up, down):
    rows, width = blocks[0].shape
    shape = jax.ShapeDtypeStruct((4, rows, width), BF)
    return pl.pallas_call(
        ffn_kernel,
        out_shape=(shape, shape),
        in_specs=[SMEM] + [VMEM] * 11,
        out_specs=(VMEM, VMEM),
        compiler_params=PARAMS,
        name="expert_ffn",
    )(order, *blocks, gate, up, down)


def fold_kernel(a, b, c, d, out):
    zs, ys, rows, width = out.shape
    total = (a[...].astype(F32) + b[...].astype(F32)) + (c[...].astype(F32) + d[...].astype(F32))
    for y in range(ys):
        part = total[:, y * width : (y + 1) * width]
        out[:, y] = part.reshape(zs, rows, width).astype(BF)


def fold(parts, zs, ys):
    rows, width = parts[0].shape
    return pl.pallas_call(
        fold_kernel,
        out_shape=jax.ShapeDtypeStruct((zs, ys, rows // zs, width // ys), BF),
        in_specs=[VMEM] * 4,
        out_specs=VMEM,
        compiler_params=PARAMS,
        name="sum_and_split",
    )(*parts)


def project_kernel(order, *refs):
    blocks, projector, outs = refs[:8], refs[8], refs[9:]
    total = jnp.zeros((blocks[0].shape[0], projector.shape[2]), F32)
    for k in range(8):
        total += jnp.dot(blocks[k][...], projector[order[k]], preferred_element_type=F32)
    rows = outs[0].shape[0]
    for i, out in enumerate(outs):
        out[...] = total[i * rows : (i + 1) * rows].astype(out.dtype)


def project(order, blocks, projector):
    tokens, cols = blocks[0].shape[0] // 4, projector.shape[2]
    return pl.pallas_call(
        project_kernel,
        out_shape=[jax.ShapeDtypeStruct((tokens, cols), F32)]
        + [jax.ShapeDtypeStruct((tokens, cols), BF)] * 3,
        in_specs=[SMEM] + [VMEM] * 9,
        out_specs=[VMEM] * 4,
        compiler_params=PARAMS,
        name="project",
    )(order, *blocks, projector)


def gradient_kernel(order, *refs):
    blocks, inputs_t, outs, errors, total = refs[:8], refs[8], refs[9:13], refs[13], refs[14]
    tokens = blocks[0].shape[0]
    for k in range(8):
        errors[pl.ds(pl.multiple_of(order[k] * tokens, 128), tokens), :] = blocks[k][...]
    total[...] = jnp.dot(inputs_t[...], errors[...], preferred_element_type=F32)
    rows = outs[0].shape[0]
    for i, out in enumerate(outs):
        out[...] = total[pl.ds(pl.multiple_of(order[8 + i] * rows, 32), rows), :].astype(out.dtype)


def gradient_parts(order, blocks, inputs_t):
    tokens, cols = blocks[0].shape
    rows = inputs_t.shape[0]
    return pl.pallas_call(
        gradient_kernel,
        out_shape=[jax.ShapeDtypeStruct((rows // 4, cols), F32)]
        + [jax.ShapeDtypeStruct((rows // 4, cols), BF)] * 3,
        in_specs=[SMEM] + [VMEM] * 9,
        out_specs=[VMEM] * 4,
        scratch_shapes=[pltpu.VMEM((8 * tokens, cols), BF), pltpu.VMEM((rows, cols), F32)],
        compiler_params=PARAMS,
        name="gradient",
    )(order, *blocks, inputs_t)


def body(
    teacher_tokens,
    routes,
    slots,
    route_weights,
    gate_proj,
    up_proj,
    down_proj,
    projector,
    student_input,
    student_weight,
):
    fsdp = ("z", "y")
    zs, ys = lax.axis_size("z"), lax.axis_size("y")
    x, c, z, y = (lax.axis_index(name) for name in ("x", "c", "z", "y"))
    owners = zs * ys
    tokens, model = teacher_tokens.shape
    width = model // 8
    slot_count = owners * CAP
    chips = (x + jnp.arange(4, dtype=jnp.int32)) % 4
    order = jnp.concatenate([chips * 2 + c, chips * 2 + (1 - c)])

    slot_index = jnp.where(routes < owners, routes * CAP + slots, -1).T
    slot_ids = jnp.arange(slot_count, dtype=jnp.int32)[:, None]
    mask = jnp.zeros((slot_count, tokens), F32)
    for k in range(slot_index.shape[0]):
        mask = mask + (slot_index[k][None, :] == slot_ids).astype(F32)
    my_cols = lax.dynamic_slice_in_dim(teacher_tokens, (x * 2 + c) * width, width, 1)
    outgoing = jnp.dot(mask.astype(BF), my_cols, preferred_element_type=F32).astype(BF)
    arrived = lax.all_to_all(
        outgoing.reshape(owners, CAP, width), fsdp, split_axis=0, concat_axis=0, tiled=True
    ).reshape(slot_count, width)

    projector_z = lax.all_gather(projector, "z", axis=0, tiled=True).reshape(
        zs, projector.shape[0], projector.shape[1]
    )
    weight_y = [student_weight] + [shifted(student_weight, "y", hop) for hop in (1, 2, 3)]
    weight_y = lax.dynamic_slice_in_dim(jnp.stack(weight_y * 2), (4 - y) % 4, 4, 0)
    weight_y = weight_y.reshape(ys * student_weight.shape[0], student_weight.shape[1])
    input_cols = student_input.shape[1] // zs
    inputs_z = lax.all_to_all(
        student_input.reshape(tokens, zs, input_cols).transpose(1, 0, 2),
        "z",
        split_axis=0,
        concat_axis=0,
        tiled=True,
    ).reshape(zs * tokens, input_cols)
    inputs_t = inputs_z.T
    student_part = jnp.dot(inputs_z, weight_y, preferred_element_type=F32).astype(BF)
    student_out = lax.psum_scatter(student_part, "z", scatter_dimension=0, tiled=True)

    row_index = jnp.where(routes < owners, routes * (ys * CAP) + slots, -1).T
    packed = jnp.concatenate([row_index.astype(F32), route_weights.T])
    combine_rows = []
    row_ids = jnp.arange(slot_count * ys, dtype=jnp.int32)[None, :]
    for hop in range(ys):
        plan = packed if hop == 0 else shifted(packed, "y", hop)
        base = ((y + hop) % ys) * CAP
        part = jnp.zeros((tokens, slot_count * ys), F32)
        for k in range(8):
            row = plan[k].astype(jnp.int32)
            row = jnp.where(row >= 0, row + base, -1)
            part = part + jnp.where(row[:, None] == row_ids, plan[8 + k][:, None], 0.0)
        combine_rows.append(part)
    combine = jnp.concatenate(combine_rows)
    combine_high = lax.reduce_precision(combine, 8, 7)
    combine_low = (combine - combine_high).astype(BF)
    combine_high = combine_high.astype(BF)

    blocks = gather_expert(arrived)
    keep, send = ffn(order, blocks, gate_proj[0], up_proj[0], down_proj[0])
    taken = shifted(send, "c", 1)
    pairs = [(keep[i].astype(F32) + taken[i].astype(F32)).astype(BF) for i in range(4)]
    parts = [pairs[0]] + [shifted(pairs[hop], "x", -hop) for hop in (1, 2, 3)]
    outgoing_rows = fold(parts, zs, ys)
    returned = lax.all_to_all(
        outgoing_rows.reshape(owners, ys * CAP, width // ys),
        fsdp,
        split_axis=0,
        concat_axis=0,
        tiled=True,
    ).reshape(slot_count * ys, width // ys)
    teacher = (
        jnp.dot(combine_high, returned, preferred_element_type=F32)
        + jnp.dot(combine_low, returned, preferred_element_type=F32)
    ).astype(BF)

    sums = project(order, gather_expert(teacher), projector_z)
    projected = sums[0]
    for hop in (1, 2, 3):
        projected = projected + shifted(sums[hop], "y", -hop).astype(F32)
    scale = 1.0 / math.sqrt(tokens * owners)
    error = ((student_out.astype(F32) - projected) * scale).astype(BF)

    ahead, behind = [error], [error]
    for hop in (1, 2, 3, 4):
        ahead.append(shifted(ahead[-1], "z", 1))
        if hop < 4:
            behind.append(shifted(behind[-1], "z", -1))
    errors = [error] + ahead[1:] + behind[1:]
    spots = jnp.array([0, 1, 2, 3, 4, -1, -2, -3], jnp.int32)
    grad_order = jnp.concatenate([(z + spots) % zs, (y + jnp.arange(4, dtype=jnp.int32)) % ys])
    grads = gradient_parts(grad_order, errors, inputs_t)
    gradient = grads[0]
    for hop in (1, 2, 3):
        gradient = gradient + shifted(grads[hop], "y", -hop).astype(F32)
    return (projected.astype(BF), gradient)


def solution(mesh):
    fine = Mesh(mesh.devices.reshape(4, 2, 8, 4), ("x", "c", "z", "y"))
    fsdp, expert = ("z", "y"), ("x", "c")
    return jax.shard_map(
        body,
        mesh=fine,
        in_specs=(
            P(fsdp, None),
            P(fsdp, None),
            P(fsdp, None),
            P(fsdp, None),
            P(fsdp, None, expert),
            P(fsdp, None, expert),
            P(fsdp, expert, None),
            P(fsdp, expert),
            P(fsdp, None),
            P(fsdp, expert),
        ),
        out_specs=(P(fsdp, expert), P(fsdp, expert)),
        check_vma=False,
    )
```

```python
import math

import jax
import jax.numpy as jnp
from jax import lax
from jax.experimental import pallas as pl
from jax.experimental.pallas import tpu as pltpu
from jax.sharding import Mesh
from jax.sharding import PartitionSpec as P

CAP = 4
BF = jnp.bfloat16
F32 = jnp.float32
VMEM = pl.BlockSpec(memory_space=pltpu.VMEM)
SMEM = pl.BlockSpec(memory_space=pltpu.SMEM)


def limit(mib):
    return pltpu.CompilerParams(vmem_limit_bytes=mib * 1024 * 1024)


def after(value, *earlier):
    return lax.optimization_barrier((value, *earlier))[0]


def in_hbm(value):
    return pltpu.with_memory_space_constraint(value, pltpu.HBM)


def shifted(value, axis, hop):
    size = lax.axis_size(axis)
    return lax.ppermute(value, axis, [(i, (i - hop) % size) for i in range(size)])


def gather_expert(value):
    own = [value] + [shifted(value, "x", hop) for hop in (1, 2, 3)]
    other = [shifted(block, "c", 1) for block in own]
    return own + other


def ffn_kernel(order, *refs):
    blocks, hbm, (keep, send), (gate, up, down, sems) = refs[:8], refs[8:11], refs[11:13], refs[13:]
    width = blocks[0].shape[1]

    def rows(k):
        return pl.ds(pl.multiple_of(order[k] * width, 128), width)

    copies = [
        pltpu.make_async_copy(hbm[i].at[rows(k), :], target.at[rows(k), :], sems.at[2 * k + i])
        for k in range(8)
        for i, target in enumerate((gate, up))
    ] + [pltpu.make_async_copy(hbm[2], down, sems.at[16])]
    for copy in copies:
        copy.start()
    gate_act = jnp.zeros((blocks[0].shape[0], gate.shape[1]), F32)
    up_act = jnp.zeros_like(gate_act)
    for k in range(8):
        copies[2 * k].wait()
        copies[2 * k + 1].wait()
        block = blocks[k][...]
        gate_act += jnp.dot(block, gate[rows(k), :], preferred_element_type=F32)
        up_act += jnp.dot(block, up[rows(k), :], preferred_element_type=F32)
    copies[16].wait()
    hidden = (gate_act / (1.0 + jnp.exp(-gate_act)) * up_act).astype(BF)
    for k in (4, 5, 6, 7, 0, 1, 2, 3):
        cols = pl.ds(pl.multiple_of(order[k] * width, 128), width)
        part = jnp.dot(hidden, down[:, cols], preferred_element_type=F32).astype(BF)
        if k < 4:
            keep[k] = part
        else:
            send[k - 4] = part


def ffn(order, blocks, gate, up, down):
    rows, width = blocks[0].shape
    shape = jax.ShapeDtypeStruct((4, rows, width), BF)
    return pl.pallas_call(
        ffn_kernel,
        out_shape=(shape, shape),
        in_specs=[SMEM] + [VMEM] * 8 + [pl.BlockSpec(memory_space=pltpu.HBM)] * 3,
        out_specs=(VMEM, VMEM),
        scratch_shapes=[pltpu.VMEM(weight.shape, BF) for weight in (gate, up, down)]
        + [pltpu.SemaphoreType.DMA((17,))],
        compiler_params=limit(16),
        name="expert_ffn",
    )(order, *blocks, in_hbm(gate), in_hbm(up), in_hbm(down))


def fold_kernel(a, b, c, d, out):
    zs, ys, rows, width = out.shape
    total = (a[...].astype(F32) + b[...].astype(F32)) + (c[...].astype(F32) + d[...].astype(F32))
    for y in range(ys):
        part = total[:, y * width : (y + 1) * width]
        out[:, y] = part.reshape(zs, rows, width).astype(BF)


def fold(parts, zs, ys):
    rows, width = parts[0].shape
    return pl.pallas_call(
        fold_kernel,
        out_shape=jax.ShapeDtypeStruct((zs, ys, rows // zs, width // ys), BF),
        in_specs=[VMEM] * 4,
        out_specs=VMEM,
        compiler_params=limit(8),
        name="sum_and_split",
    )(*parts)


def project_kernel(order, *refs):
    blocks, projector, outs = refs[:8], refs[8], refs[9:]
    total = jnp.zeros((blocks[0].shape[0], projector.shape[2]), F32)
    for k in range(8):
        total += jnp.dot(blocks[k][...], projector[order[k]], preferred_element_type=F32)
    rows = outs[0].shape[0]
    for i, out in enumerate(outs):
        out[...] = total[i * rows : (i + 1) * rows].astype(out.dtype)


def project(order, blocks, projector):
    tokens, cols = blocks[0].shape[0] // 4, projector.shape[2]
    return pl.pallas_call(
        project_kernel,
        out_shape=[jax.ShapeDtypeStruct((tokens, cols), F32)]
        + [jax.ShapeDtypeStruct((tokens, cols), BF)] * 3,
        in_specs=[SMEM] + [VMEM] * 9,
        out_specs=[VMEM] * 4,
        compiler_params=limit(12),
        name="project",
    )(order, *blocks, projector)


def gradient_kernel(order, *refs):
    blocks, inputs_t, outs, errors, total = refs[:8], refs[8], refs[9:13], refs[13], refs[14]
    tokens = blocks[0].shape[0]
    for k in range(8):
        errors[pl.ds(pl.multiple_of(order[k] * tokens, 128), tokens), :] = blocks[k][...]
    total[...] = jnp.dot(inputs_t[...], errors[...], preferred_element_type=F32)
    rows = outs[0].shape[0]
    for i, out in enumerate(outs):
        out[...] = total[pl.ds(pl.multiple_of(order[8 + i] * rows, 32), rows), :].astype(out.dtype)


def gradient_parts(order, blocks, inputs_t):
    tokens, cols = blocks[0].shape
    rows = inputs_t.shape[0]
    return pl.pallas_call(
        gradient_kernel,
        out_shape=[jax.ShapeDtypeStruct((rows // 4, cols), F32)]
        + [jax.ShapeDtypeStruct((rows // 4, cols), BF)] * 3,
        in_specs=[SMEM] + [VMEM] * 9,
        out_specs=[VMEM] * 4,
        scratch_shapes=[pltpu.VMEM((8 * tokens, cols), BF), pltpu.VMEM((rows, cols), F32)],
        compiler_params=limit(16),
        name="gradient",
    )(order, *blocks, inputs_t)


def student_kernel(order, *refs):
    halves, gathered, part, inputs, weight = refs[:2], refs[2], refs[3], refs[4], refs[5]
    tokens = halves[0].shape[1]
    for k in range(2):
        inputs[:, pl.ds(pl.multiple_of(order[k] * tokens, 32), tokens), :] = halves[k][...]
    rows = weight.shape[0] // 4
    for k in range(4):
        weight[k * rows : (k + 1) * rows, :] = gathered[k, :rows, :]
    flat = inputs[...].reshape(part.shape[0], weight.shape[0])
    part[...] = jnp.dot(flat, weight[...], preferred_element_type=F32).astype(BF)


def student(order, halves, gathered):
    zs, tokens, width = halves[0].shape
    cols = gathered.shape[2]
    return pl.pallas_call(
        student_kernel,
        out_shape=(
            jax.ShapeDtypeStruct((zs * 2 * tokens, cols), BF),
            jax.ShapeDtypeStruct((zs, 2 * tokens, width), BF),
        ),
        in_specs=[SMEM] + [VMEM] * 3,
        out_specs=(VMEM, VMEM),
        scratch_shapes=[pltpu.VMEM((width, cols), BF)],
        compiler_params=limit(16),
        name="student",
    )(order, *halves, gathered)


def body(
    teacher_tokens,
    routes,
    slots,
    route_weights,
    gate_proj,
    up_proj,
    down_proj,
    projector,
    student_input,
    student_weight,
):
    fsdp = ("z", "y")
    zs, ys = lax.axis_size("z"), lax.axis_size("y")
    x, c, z, y = (lax.axis_index(name) for name in ("x", "c", "z", "y"))
    owners = zs * ys
    tokens, model = teacher_tokens.shape
    width = model // 8
    slot_count = owners * CAP
    chips = (x + jnp.arange(4, dtype=jnp.int32)) % 4
    order = jnp.concatenate([chips * 2 + c, chips * 2 + (1 - c)])

    weight_rows = student_weight.shape[0]
    in_wave = (routes < owners).T
    high = lax.reduce_precision(route_weights.T, 8, 7)
    info = jnp.concatenate(
        [jnp.where(in_wave, routes.T, -64), jnp.where(in_wave, slots.T, 0), high, route_weights.T - high]
    ).astype(BF)
    info = jnp.pad(info, ((0, 16), (0, student_weight.shape[1] - tokens)))
    weight_info = jnp.concatenate([student_weight, info])
    gathered = lax.all_gather(weight_info, "y", axis=0)

    slot_index = jnp.where(routes < owners, routes * CAP + slots, -1).T
    slot_ids = jnp.arange(slot_count, dtype=jnp.int32)[:, None]
    mask = jnp.zeros((slot_count, tokens), F32)
    for k in range(slot_index.shape[0]):
        mask = mask + (slot_index[k][None, :] == slot_ids).astype(F32)
    my_cols = lax.dynamic_slice_in_dim(teacher_tokens, (x * 2 + c) * width, width, 1)
    outgoing = jnp.dot(mask.astype(BF), my_cols, preferred_element_type=F32).astype(BF)
    outgoing = after(outgoing, weight_info)
    arrived = lax.all_to_all(
        outgoing.reshape(owners, CAP, width), fsdp, split_axis=0, concat_axis=0, tiled=True
    ).reshape(slot_count, width)

    projector_z = lax.all_gather(after(projector, weight_info), "z", axis=0, tiled=True).reshape(
        zs, projector.shape[0], projector.shape[1]
    )
    plans = gathered[:, weight_rows : weight_rows + 32, :tokens].astype(F32)
    plans = lax.dynamic_slice_in_dim(jnp.concatenate([plans, plans]), y, ys, 0)
    combine_rows = []
    row_ids = jnp.arange(slot_count * ys, dtype=jnp.int32)[None, :]
    for hop in range(ys):
        plan = plans[hop]
        place = plan[:8] * (ys * CAP) + plan[8:16] + (((y + hop) % ys) * CAP).astype(F32)
        place, share = place.astype(jnp.int32), plan[16:24] + plan[24:32]
        part = jnp.zeros((tokens, slot_count * ys), F32)
        for k in range(8):
            part = part + jnp.where(place[k][:, None] == row_ids, share[k][:, None], 0.0)
        combine_rows.append(part)
    combine = jnp.concatenate(combine_rows)
    combine_high = lax.reduce_precision(combine, 8, 7)
    combine_low = (combine - combine_high).astype(BF)
    combine_high = combine_high.astype(BF)

    eight, four = jnp.arange(8, dtype=jnp.int32), jnp.arange(4, dtype=jnp.int32)
    spots = jnp.where(eight < 5, eight, 4 - eight)
    grad_order = jnp.concatenate([(z + spots) % zs, (y + four) % ys])
    student_order = jnp.concatenate([jnp.stack([c, 1 - c]).astype(jnp.int32)])
    tokens_half = tokens // 2
    input_cols = student_input.shape[1] // zs
    half = lax.dynamic_slice_in_dim(student_input, c * tokens_half, tokens_half, 0)
    half = half.reshape(tokens_half, zs, input_cols).transpose(1, 0, 2)
    arrived, order, grad_order, student_order, half = lax.optimization_barrier(
        (arrived, order, grad_order, student_order, half)
    )
    half = lax.all_to_all(half, "z", split_axis=0, concat_axis=0, tiled=True)

    blocks = gather_expert(arrived)
    keep, send = ffn(order, blocks, gate_proj[0], up_proj[0], down_proj[0])
    taken = shifted(send, "c", 1)
    pairs = [(keep[i].astype(F32) + taken[i].astype(F32)).astype(BF) for i in range(4)]
    parts = [pairs[0]] + [shifted(pairs[hop], "x", -hop) for hop in (1, 2, 3)]
    half = after(half, send)
    other_half = shifted(half, "c", 1)
    outgoing_rows = fold(parts, zs, ys)
    student_part, inputs_z = student(
        after(student_order, outgoing_rows), [half, other_half], gathered
    )
    inputs_t = inputs_z.reshape(zs * tokens, input_cols).T
    student_out = lax.psum_scatter(student_part, "z", scatter_dimension=0, tiled=True)
    returned = lax.all_to_all(
        outgoing_rows.reshape(owners, ys * CAP, width // ys),
        fsdp,
        split_axis=0,
        concat_axis=0,
        tiled=True,
    ).reshape(slot_count * ys, width // ys)
    returned, combine_high, combine_low = lax.optimization_barrier(
        (returned, combine_high, combine_low, inputs_t)
    )[:3]
    teacher = (
        jnp.dot(combine_high, returned, preferred_element_type=F32)
        + jnp.dot(combine_low, returned, preferred_element_type=F32)
    ).astype(BF)

    sums = project(order, gather_expert(after(teacher, projector_z)), projector_z)
    projected = sums[0]
    for hop in (1, 2, 3):
        projected = projected + shifted(sums[hop], "y", -hop).astype(F32)
    scale = 1.0 / math.sqrt(tokens * owners)
    error = ((student_out.astype(F32) - projected) * scale).astype(BF)

    ahead, behind = [error], [error]
    for hop in (1, 2, 3, 4):
        ahead.append(shifted(ahead[-1], "z", 1))
        if hop < 4:
            behind.append(shifted(behind[-1], "z", -1))
    errors = [error] + ahead[1:] + behind[1:]
    grads = gradient_parts(grad_order, errors, inputs_t)
    gradient = grads[0]
    for hop in (1, 2, 3):
        gradient = gradient + shifted(grads[hop], "y", -hop).astype(F32)
    return (projected.astype(BF), gradient)


def solution(mesh):
    fine = Mesh(mesh.devices.reshape(4, 2, 8, 4), ("x", "c", "z", "y"))
    fsdp, expert = ("z", "y"), ("x", "c")
    return jax.shard_map(
        body,
        mesh=fine,
        in_specs=(
            P(fsdp, None),
            P(fsdp, None),
            P(fsdp, None),
            P(fsdp, None),
            P(fsdp, None, expert),
            P(fsdp, None, expert),
            P(fsdp, expert, None),
            P(fsdp, expert),
            P(fsdp, None),
            P(fsdp, expert),
        ),
        out_specs=(P(fsdp, expert), P(fsdp, expert)),
        check_vma=False,
    )
```

```python
import math

import jax
import jax.numpy as jnp
from jax import lax
from jax.experimental import pallas as pl
from jax.experimental.pallas import tpu as pltpu
from jax.sharding import Mesh
from jax.sharding import PartitionSpec as P

CAP = 4
BF = jnp.bfloat16
F32 = jnp.float32
VMEM = pl.BlockSpec(memory_space=pltpu.VMEM)
SMEM = pl.BlockSpec(memory_space=pltpu.SMEM)


def limit(mib):
    return pltpu.CompilerParams(vmem_limit_bytes=mib * 1024 * 1024)


def after(value, *earlier):
    return lax.optimization_barrier((value, *earlier))[0]


def in_hbm(value):
    return pltpu.with_memory_space_constraint(value, pltpu.HBM)


def shifted(value, axis, hop):
    size = lax.axis_size(axis)
    return lax.ppermute(value, axis, [(i, (i - hop) % size) for i in range(size)])


def gather_expert(value):
    own = [value] + [shifted(value, "x", hop) for hop in (1, 2, 3)]
    other = [shifted(block, "c", 1) for block in own]
    return own + other


def ffn_kernel(order, *refs):
    blocks, hbm, (keep, send), (both, down, sems) = refs[:8], refs[8:11], refs[11:13], refs[13:]
    width = blocks[0].shape[1]
    hidden_units = down.shape[0]

    def rows(k):
        return pl.ds(pl.multiple_of(order[k] * width, 128), width)

    copies = [
        pltpu.make_async_copy(
            hbm[i].at[rows(k), :],
            both.at[rows(k), pl.ds(i * hidden_units, hidden_units)],
            sems.at[2 * k + i],
        )
        for k in range(8)
        for i in range(2)
    ] + [pltpu.make_async_copy(hbm[2], down, sems.at[16])]
    for copy in copies:
        copy.start()
    acts = jnp.zeros((blocks[0].shape[0], 2 * hidden_units), F32)
    for k in range(8):
        copies[2 * k].wait()
        copies[2 * k + 1].wait()
        acts += jnp.dot(blocks[k][...], both[rows(k), :], preferred_element_type=F32)
    gate_act, up_act = acts[:, :hidden_units], acts[:, hidden_units:]
    copies[16].wait()
    hidden = (gate_act / (1.0 + jnp.exp(-gate_act)) * up_act).astype(BF)
    for k in (4, 5, 6, 7, 0, 1, 2, 3):
        cols = pl.ds(pl.multiple_of(order[k] * width, 128), width)
        part = jnp.dot(hidden, down[:, cols], preferred_element_type=F32).astype(BF)
        if k < 4:
            keep[k] = part
        else:
            send[k - 4] = part


def ffn(order, blocks, gate, up, down):
    rows, width = blocks[0].shape
    shape = jax.ShapeDtypeStruct((4, rows, width), BF)
    return pl.pallas_call(
        ffn_kernel,
        out_shape=(shape, shape),
        in_specs=[SMEM] + [VMEM] * 8 + [pl.BlockSpec(memory_space=pltpu.HBM)] * 3,
        out_specs=(VMEM, VMEM),
        scratch_shapes=[pltpu.VMEM((gate.shape[0], 2 * gate.shape[1]), BF), pltpu.VMEM(down.shape, BF)]
        + [pltpu.SemaphoreType.DMA((17,))],
        compiler_params=limit(16),
        name="expert_ffn",
    )(order, *blocks, in_hbm(gate), in_hbm(up), in_hbm(down))


def fold_kernel(a, b, c, d, out):
    zs, ys, rows, width = out.shape
    total = (a[...].astype(F32) + b[...].astype(F32)) + (c[...].astype(F32) + d[...].astype(F32))
    for y in range(ys):
        part = total[:, y * width : (y + 1) * width]
        out[:, y] = part.reshape(zs, rows, width).astype(BF)


def fold(parts, zs, ys):
    rows, width = parts[0].shape
    return pl.pallas_call(
        fold_kernel,
        out_shape=jax.ShapeDtypeStruct((zs, ys, rows // zs, width // ys), BF),
        in_specs=[VMEM] * 4,
        out_specs=VMEM,
        compiler_params=limit(8),
        name="sum_and_split",
    )(*parts)


def load_kernel(source, target, sem):
    copy = pltpu.make_async_copy(source, target, sem)
    copy.start()
    copy.wait()


def load(value):
    return pl.pallas_call(
        load_kernel,
        out_shape=pltpu.VMEM(value.shape, value.dtype),
        in_specs=[pl.BlockSpec(memory_space=pltpu.HBM)],
        out_specs=VMEM,
        scratch_shapes=[pltpu.SemaphoreType.DMA],
        compiler_params=limit(4),
        name="load",
    )(in_hbm(value))


def project_kernel(order, *refs):
    blocks, projector, outs = refs[:8], refs[8], refs[9:]
    total = jnp.zeros((blocks[0].shape[0], projector.shape[2]), F32)
    for k in range(8):
        total += jnp.dot(blocks[k][...], projector[order[k]], preferred_element_type=F32)
    rows = outs[0].shape[0]
    for i, out in enumerate(outs):
        out[...] = total[i * rows : (i + 1) * rows].astype(out.dtype)


def project(order, blocks, projector):
    tokens, cols = blocks[0].shape[0] // 4, projector.shape[2]
    return pl.pallas_call(
        project_kernel,
        out_shape=[jax.ShapeDtypeStruct((tokens, cols), F32)]
        + [jax.ShapeDtypeStruct((tokens, cols), BF)] * 3,
        in_specs=[SMEM] + [VMEM] * 9,
        out_specs=[VMEM] * 4,
        compiler_params=limit(12),
        name="project",
    )(order, *blocks, projector)


def gradient_kernel(order, *refs):
    blocks, inputs_t, outs, errors, total = refs[:8], refs[8], refs[9:13], refs[13], refs[14]
    tokens = blocks[0].shape[0]
    for k in range(8):
        errors[pl.ds(pl.multiple_of(order[k] * tokens, 128), tokens), :] = blocks[k][...]
    total[...] = jnp.dot(inputs_t[...], errors[...], preferred_element_type=F32)
    rows = outs[0].shape[0]
    for i, out in enumerate(outs):
        out[...] = total[pl.ds(pl.multiple_of(order[8 + i] * rows, 32), rows), :].astype(out.dtype)


def gradient_parts(order, blocks, inputs_t):
    tokens, cols = blocks[0].shape
    rows = inputs_t.shape[0]
    return pl.pallas_call(
        gradient_kernel,
        out_shape=[jax.ShapeDtypeStruct((rows // 4, cols), F32)]
        + [jax.ShapeDtypeStruct((rows // 4, cols), BF)] * 3,
        in_specs=[SMEM] + [VMEM] * 9,
        out_specs=[VMEM] * 4,
        scratch_shapes=[pltpu.VMEM((8 * tokens, cols), BF), pltpu.VMEM((rows, cols), F32)],
        compiler_params=limit(16),
        name="gradient",
    )(order, *blocks, inputs_t)


def student_kernel(order, *refs):
    halves, gathered, outs, (part, inputs, weight, sems) = refs[:2], refs[2], refs[3:5], refs[5:]
    tokens = halves[0].shape[1]
    for k in range(2):
        inputs[:, pl.ds(pl.multiple_of(order[k] * tokens, 32), tokens), :] = halves[k][...]
    keep_inputs = pltpu.make_async_copy(inputs, outs[1], sems.at[0])
    keep_inputs.start()
    rows = weight.shape[0] // 4
    for k in range(4):
        weight[k * rows : (k + 1) * rows, :] = gathered[k, :rows, :]
    flat = inputs[...].reshape(part.shape[0], weight.shape[0])
    part[...] = jnp.dot(flat, weight[...], preferred_element_type=F32).astype(BF)
    keep_part = pltpu.make_async_copy(part, outs[0], sems.at[1])
    keep_part.start()
    keep_inputs.wait()
    keep_part.wait()


def student(order, halves, gathered):
    zs, tokens, width = halves[0].shape
    cols = gathered.shape[2]
    shapes = ((zs * 2 * tokens, cols), (zs, 2 * tokens, width))
    return pl.pallas_call(
        student_kernel,
        out_shape=tuple(pltpu.HBM(shape, BF) for shape in shapes),
        in_specs=[SMEM] + [VMEM] * 3,
        out_specs=(pl.BlockSpec(memory_space=pltpu.HBM),) * 2,
        scratch_shapes=[pltpu.VMEM(shape, BF) for shape in shapes]
        + [pltpu.VMEM((width, cols), BF), pltpu.SemaphoreType.DMA((2,))],
        compiler_params=limit(16),
        name="student",
    )(order, *halves, gathered)


def body(
    teacher_tokens,
    routes,
    slots,
    route_weights,
    gate_proj,
    up_proj,
    down_proj,
    projector,
    student_input,
    student_weight,
):
    fsdp = ("z", "y")
    zs, ys = lax.axis_size("z"), lax.axis_size("y")
    x, c, z, y = (lax.axis_index(name) for name in ("x", "c", "z", "y"))
    owners = zs * ys
    tokens, model = teacher_tokens.shape
    width = model // 8
    slot_count = owners * CAP
    chips = (x + jnp.arange(4, dtype=jnp.int32)) % 4
    order = jnp.concatenate([chips * 2 + c, chips * 2 + (1 - c)])

    weight_rows = student_weight.shape[0]
    in_wave = (routes < owners).T
    high = lax.reduce_precision(route_weights.T, 8, 7)
    info = jnp.concatenate(
        [jnp.where(in_wave, routes.T, -64), jnp.where(in_wave, slots.T, 0), high, route_weights.T - high]
    ).astype(BF)
    info = jnp.pad(info, ((0, 16), (0, student_weight.shape[1] - tokens)))
    weight_info = jnp.concatenate([student_weight, info])
    gathered = lax.all_gather(weight_info, "y", axis=0)

    slot_index = jnp.where(routes < owners, routes * CAP + slots, -1).T
    slot_ids = jnp.arange(slot_count, dtype=jnp.int32)[:, None]
    mask = jnp.zeros((slot_count, tokens), F32)
    for k in range(slot_index.shape[0]):
        mask = mask + (slot_index[k][None, :] == slot_ids).astype(F32)
    my_cols = lax.dynamic_slice_in_dim(teacher_tokens, (x * 2 + c) * width, width, 1)
    outgoing = jnp.dot(mask.astype(BF), my_cols, preferred_element_type=F32).astype(BF)
    outgoing = after(outgoing, weight_info)
    arrived = lax.all_to_all(
        outgoing.reshape(owners, CAP, width), fsdp, split_axis=0, concat_axis=0, tiled=True
    ).reshape(slot_count, width)

    projector_z = lax.all_gather(after(projector, weight_info), "z", axis=0, tiled=True).reshape(
        zs, projector.shape[0], projector.shape[1]
    )
    plans = gathered[:, weight_rows : weight_rows + 32, :tokens].astype(F32)
    plans = lax.dynamic_slice_in_dim(jnp.concatenate([plans, plans]), y, ys, 0)
    combine_rows = []
    row_ids = jnp.arange(slot_count * ys, dtype=jnp.int32)[None, :]
    for hop in range(ys):
        plan = plans[hop]
        place = plan[:8] * (ys * CAP) + plan[8:16] + (((y + hop) % ys) * CAP).astype(F32)
        place, share = place.astype(jnp.int32), plan[16:24] + plan[24:32]
        part = jnp.zeros((tokens, slot_count * ys), F32)
        for k in range(8):
            part = part + jnp.where(place[k][:, None] == row_ids, share[k][:, None], 0.0)
        combine_rows.append(part)
    combine = jnp.concatenate(combine_rows)
    combine = combine.astype(BF)

    eight, four = jnp.arange(8, dtype=jnp.int32), jnp.arange(4, dtype=jnp.int32)
    spots = jnp.where(eight < 5, eight, 4 - eight)
    grad_order = jnp.concatenate([(z + spots) % zs, (y + four) % ys])
    student_order = jnp.concatenate([jnp.stack([c, 1 - c]).astype(jnp.int32)])
    tokens_half = tokens // 2
    input_cols = student_input.shape[1] // zs
    half = lax.dynamic_slice_in_dim(student_input, c * tokens_half, tokens_half, 0)
    half = half.reshape(tokens_half, zs, input_cols).transpose(1, 0, 2)
    arrived, order, grad_order, student_order, half = lax.optimization_barrier(
        (arrived, order, grad_order, student_order, half)
    )
    half = lax.all_to_all(half, "z", split_axis=0, concat_axis=0, tiled=True)

    blocks = gather_expert(arrived)
    keep, send = ffn(order, blocks, gate_proj[0], up_proj[0], down_proj[0])
    taken = shifted(send, "c", 1)
    pairs = [(keep[i].astype(F32) + taken[i].astype(F32)).astype(BF) for i in range(4)]
    parts = [pairs[0]] + [shifted(pairs[hop], "x", -hop) for hop in (1, 2, 3)]
    half = after(half, send)
    other_half = shifted(half, "c", 1)
    outgoing_rows = fold(parts, zs, ys)
    student_part, inputs_z = student(
        after(student_order, outgoing_rows), [half, other_half], gathered
    )
    inputs_t = inputs_z.reshape(zs * tokens, input_cols).T
    student_out = lax.psum_scatter(student_part, "z", scatter_dimension=0, tiled=True)
    returned = lax.all_to_all(
        outgoing_rows.reshape(owners, ys * CAP, width // ys),
        fsdp,
        split_axis=0,
        concat_axis=0,
        tiled=True,
    ).reshape(slot_count * ys, width // ys)
    returned, combine = lax.optimization_barrier((returned, combine, inputs_t))[:2]
    teacher = jnp.dot(combine, returned, preferred_element_type=F32).astype(BF)

    teacher = after(teacher, projector_z)
    sums = project(order, gather_expert(teacher), load(after(projector_z, teacher)))
    projected = sums[0]
    for hop in (1, 2, 3):
        projected = projected + shifted(sums[hop], "y", -hop).astype(F32)
    scale = 1.0 / math.sqrt(tokens * owners)
    error = ((student_out.astype(F32) - projected) * scale).astype(BF)

    ahead, behind = [error], [error]
    for hop in (1, 2, 3, 4):
        ahead.append(shifted(ahead[-1], "z", 1))
        if hop < 4:
            behind.append(shifted(behind[-1], "z", -1))
    errors = [error] + ahead[1:] + behind[1:]
    grads = gradient_parts(grad_order, errors, inputs_t)
    gradient = grads[0]
    for hop in (1, 2, 3):
        gradient = gradient + shifted(grads[hop], "y", -hop).astype(F32)
    return (projected.astype(BF), gradient)


def solution(mesh):
    fine = Mesh(mesh.devices.reshape(4, 2, 8, 4), ("x", "c", "z", "y"))
    fsdp, expert = ("z", "y"), ("x", "c")
    return jax.shard_map(
        body,
        mesh=fine,
        in_specs=(
            P(fsdp, None),
            P(fsdp, None),
            P(fsdp, None),
            P(fsdp, None),
            P(fsdp, None, expert),
            P(fsdp, None, expert),
            P(fsdp, expert, None),
            P(fsdp, expert),
            P(fsdp, None),
            P(fsdp, expert),
        ),
        out_specs=(P(fsdp, expert), P(fsdp, expert)),
        check_vma=False,
    )
```

```python
import math

import jax
import jax.numpy as jnp
from jax import lax
from jax.experimental import pallas as pl
from jax.experimental.pallas import tpu as pltpu
from jax.sharding import Mesh
from jax.sharding import PartitionSpec as P

CAP = 4
BF = jnp.bfloat16
F32 = jnp.float32
VMEM = pl.BlockSpec(memory_space=pltpu.VMEM)
SMEM = pl.BlockSpec(memory_space=pltpu.SMEM)


def limit(mib):
    return pltpu.CompilerParams(vmem_limit_bytes=mib * 1024 * 1024)


def after(value, *earlier):
    return lax.optimization_barrier((value, *earlier))[0]


def in_hbm(value):
    return pltpu.with_memory_space_constraint(value, pltpu.HBM)


def shifted(value, axis, hop):
    size = lax.axis_size(axis)
    return lax.ppermute(value, axis, [(i, (i - hop) % size) for i in range(size)])


def gather_expert(value):
    own = [value] + [shifted(value, "x", hop) for hop in (1, 2, 3)]
    other = [shifted(block, "c", 1) for block in own]
    return own + other


def ffn_kernel(order, *refs):
    blocks, hbm, (keep, send), (both, down, sems) = refs[:8], refs[8:11], refs[11:13], refs[13:]
    width = blocks[0].shape[1]
    hidden_units = down.shape[0]

    def rows(k):
        return pl.ds(pl.multiple_of(order[k] * width, 128), width)

    copies = [
        pltpu.make_async_copy(
            hbm[i].at[rows(k), :],
            both.at[rows(k), pl.ds(i * hidden_units, hidden_units)],
            sems.at[2 * k + i],
        )
        for k in range(8)
        for i in range(2)
    ] + [pltpu.make_async_copy(hbm[2], down, sems.at[16])]
    for copy in copies:
        copy.start()
    acts = jnp.zeros((blocks[0].shape[0], 2 * hidden_units), F32)
    for k in range(8):
        copies[2 * k].wait()
        copies[2 * k + 1].wait()
        acts += jnp.dot(blocks[k][...], both[rows(k), :], preferred_element_type=F32)
    gate_act, up_act = acts[:, :hidden_units], acts[:, hidden_units:]
    copies[16].wait()
    hidden = (gate_act / (1.0 + jnp.exp(-gate_act)) * up_act).astype(BF)
    for k in (4, 5, 6, 7, 0, 1, 2, 3):
        cols = pl.ds(pl.multiple_of(order[k] * width, 128), width)
        part = jnp.dot(hidden, down[:, cols], preferred_element_type=F32).astype(BF)
        if k < 4:
            keep[k] = part
        else:
            send[k - 4] = part


def ffn(order, blocks, gate, up, down):
    rows, width = blocks[0].shape
    shape = jax.ShapeDtypeStruct((4, rows, width), BF)
    return pl.pallas_call(
        ffn_kernel,
        out_shape=(shape, shape),
        in_specs=[SMEM] + [VMEM] * 8 + [pl.BlockSpec(memory_space=pltpu.HBM)] * 3,
        out_specs=(VMEM, VMEM),
        scratch_shapes=[pltpu.VMEM((gate.shape[0], 2 * gate.shape[1]), BF), pltpu.VMEM(down.shape, BF)]
        + [pltpu.SemaphoreType.DMA((17,))],
        compiler_params=limit(16),
        name="expert_ffn",
    )(order, *blocks, in_hbm(gate), in_hbm(up), in_hbm(down))


def fold_kernel(a, b, c, d, out):
    zs, ys, rows, width = out.shape
    total = (a[...].astype(F32) + b[...].astype(F32)) + (c[...].astype(F32) + d[...].astype(F32))
    for y in range(ys):
        part = total[:, y * width : (y + 1) * width]
        out[:, y] = part.reshape(zs, rows, width).astype(BF)


def fold(parts, zs, ys):
    rows, width = parts[0].shape
    return pl.pallas_call(
        fold_kernel,
        out_shape=jax.ShapeDtypeStruct((zs, ys, rows // zs, width // ys), BF),
        in_specs=[VMEM] * 4,
        out_specs=VMEM,
        compiler_params=limit(8),
        name="sum_and_split",
    )(*parts)


def load_kernel(source, target, sem):
    copy = pltpu.make_async_copy(source, target, sem)
    copy.start()
    copy.wait()


def load(value):
    return pl.pallas_call(
        load_kernel,
        out_shape=pltpu.VMEM(value.shape, value.dtype),
        in_specs=[pl.BlockSpec(memory_space=pltpu.HBM)],
        out_specs=VMEM,
        scratch_shapes=[pltpu.SemaphoreType.DMA],
        compiler_params=limit(4),
        name="load",
    )(in_hbm(value))


def project_kernel(order, *refs):
    blocks, projector, outs = refs[:8], refs[8], refs[9:]
    total = jnp.zeros((blocks[0].shape[0], projector.shape[2]), F32)
    for k in range(8):
        total += jnp.dot(blocks[k][...], projector[order[k]], preferred_element_type=F32)
    rows = outs[0].shape[0]
    for i, out in enumerate(outs):
        out[...] = total[i * rows : (i + 1) * rows].astype(out.dtype)


def project(order, blocks, projector):
    tokens, cols = blocks[0].shape[0] // 4, projector.shape[2]
    return pl.pallas_call(
        project_kernel,
        out_shape=[jax.ShapeDtypeStruct((tokens, cols), F32)]
        + [jax.ShapeDtypeStruct((tokens, cols), BF)] * 3,
        in_specs=[SMEM] + [VMEM] * 9,
        out_specs=[VMEM] * 4,
        compiler_params=limit(12),
        name="project",
    )(order, *blocks, projector)


def gradient_kernel(order, *refs):
    blocks, inputs_t, outs, errors, total = refs[:8], refs[8], refs[9:13], refs[13], refs[14]
    tokens = blocks[0].shape[0]
    for k in range(8):
        errors[pl.ds(pl.multiple_of(order[k] * tokens, 128), tokens), :] = blocks[k][...]
    total[...] = jnp.dot(inputs_t[...], errors[...], preferred_element_type=F32)
    rows = outs[0].shape[0]
    for i, out in enumerate(outs):
        out[...] = total[pl.ds(pl.multiple_of(order[8 + i] * rows, 32), rows), :].astype(out.dtype)


def gradient_parts(order, blocks, inputs_t):
    tokens, cols = blocks[0].shape
    rows = inputs_t.shape[0]
    return pl.pallas_call(
        gradient_kernel,
        out_shape=[jax.ShapeDtypeStruct((rows // 4, cols), F32)]
        + [jax.ShapeDtypeStruct((rows // 4, cols), BF)] * 3,
        in_specs=[SMEM] + [VMEM] * 9,
        out_specs=[VMEM] * 4,
        scratch_shapes=[pltpu.VMEM((8 * tokens, cols), BF), pltpu.VMEM((rows, cols), F32)],
        compiler_params=limit(16),
        name="gradient",
    )(order, *blocks, inputs_t)


def student_kernel(order, *refs):
    halves, gathered, outs, (part, inputs, weight, sems) = refs[:2], refs[2], refs[3:5], refs[5:]
    tokens = halves[0].shape[1]
    for k in range(2):
        inputs[:, pl.ds(pl.multiple_of(order[k] * tokens, 32), tokens), :] = halves[k][...]
    keep_inputs = pltpu.make_async_copy(inputs, outs[1], sems.at[0])
    keep_inputs.start()
    rows = weight.shape[0] // 4
    for k in range(4):
        weight[k * rows : (k + 1) * rows, :] = gathered[k, :rows, :]
    flat = inputs[...].reshape(part.shape[0], weight.shape[0])
    part[...] = jnp.dot(flat, weight[...], preferred_element_type=F32).astype(BF)
    keep_part = pltpu.make_async_copy(part, outs[0], sems.at[1])
    keep_part.start()
    keep_inputs.wait()
    keep_part.wait()


def student(order, halves, gathered):
    zs, tokens, width = halves[0].shape
    cols = gathered.shape[2]
    shapes = ((zs * 2 * tokens, cols), (zs, 2 * tokens, width))
    return pl.pallas_call(
        student_kernel,
        out_shape=tuple(pltpu.HBM(shape, BF) for shape in shapes),
        in_specs=[SMEM] + [VMEM] * 3,
        out_specs=(pl.BlockSpec(memory_space=pltpu.HBM),) * 2,
        scratch_shapes=[pltpu.VMEM(shape, BF) for shape in shapes]
        + [pltpu.VMEM((width, cols), BF), pltpu.SemaphoreType.DMA((2,))],
        compiler_params=limit(16),
        name="student",
    )(order, *halves, gathered)


def body(
    teacher_tokens,
    routes,
    slots,
    route_weights,
    gate_proj,
    up_proj,
    down_proj,
    projector,
    student_input,
    student_weight,
):
    fsdp = ("z", "y")
    zs, ys = lax.axis_size("z"), lax.axis_size("y")
    x, c, z, y = (lax.axis_index(name) for name in ("x", "c", "z", "y"))
    owners = zs * ys
    tokens, model = teacher_tokens.shape
    width = model // 8
    slot_count = owners * CAP
    chips = (x + jnp.arange(4, dtype=jnp.int32)) % 4
    order = jnp.concatenate([chips * 2 + c, chips * 2 + (1 - c)])

    weight_rows = student_weight.shape[0]
    in_wave = (routes < owners).T
    info = jnp.concatenate(
        [jnp.where(in_wave, routes.T, -64), jnp.where(in_wave, slots.T, 0), route_weights.T]
    ).astype(BF)
    info = jnp.pad(info, ((0, 24), (0, student_weight.shape[1] - tokens)))
    weight_info = jnp.concatenate([student_weight, info])
    gathered = lax.all_gather(weight_info, "y", axis=0)

    slot_index = jnp.where(routes < owners, routes * CAP + slots, -1).T
    slot_ids = jnp.arange(slot_count, dtype=jnp.int32)[:, None]
    mask = jnp.zeros((slot_count, tokens), F32)
    for k in range(slot_index.shape[0]):
        mask = mask + (slot_index[k][None, :] == slot_ids).astype(F32)
    my_cols = lax.dynamic_slice_in_dim(teacher_tokens, (x * 2 + c) * width, width, 1)
    outgoing = jnp.dot(mask.astype(BF), my_cols, preferred_element_type=F32).astype(BF)
    outgoing = after(outgoing, weight_info)
    arrived = lax.all_to_all(
        outgoing.reshape(owners, CAP, width), fsdp, split_axis=0, concat_axis=0, tiled=True
    ).reshape(slot_count, width)

    projector_z = lax.all_gather(after(projector, weight_info), "z", axis=0, tiled=True).reshape(
        zs, projector.shape[0], projector.shape[1]
    )
    plans = gathered[:, weight_rows : weight_rows + 24, :tokens].astype(F32)
    plans = lax.dynamic_slice_in_dim(jnp.concatenate([plans, plans]), y, ys, 0)
    combine_rows = []
    row_ids = jnp.arange(slot_count * ys, dtype=jnp.int32)[None, :]
    for hop in range(ys):
        plan = plans[hop]
        place = plan[:8] * (ys * CAP) + plan[8:16] + (((y + hop) % ys) * CAP).astype(F32)
        place, share = place.astype(jnp.int32), plan[16:24]
        part = jnp.zeros((tokens, slot_count * ys), F32)
        for k in range(8):
            part = part + jnp.where(place[k][:, None] == row_ids, share[k][:, None], 0.0)
        combine_rows.append(part)
    combine = jnp.concatenate(combine_rows)
    combine = combine.astype(BF)

    eight, four = jnp.arange(8, dtype=jnp.int32), jnp.arange(4, dtype=jnp.int32)
    spots = jnp.where(eight < 5, eight, 4 - eight)
    grad_order = jnp.concatenate([(z + spots) % zs, (y + four) % ys])
    student_order = jnp.concatenate([jnp.stack([c, 1 - c]).astype(jnp.int32)])
    tokens_half = tokens // 2
    input_cols = student_input.shape[1] // zs
    half = lax.dynamic_slice_in_dim(student_input, c * tokens_half, tokens_half, 0)
    half = half.reshape(tokens_half, zs, input_cols).transpose(1, 0, 2)
    arrived, order, grad_order, student_order, half = lax.optimization_barrier(
        (arrived, order, grad_order, student_order, half)
    )
    half = lax.all_to_all(half, "z", split_axis=0, concat_axis=0, tiled=True)

    blocks = gather_expert(arrived)
    keep, send = ffn(order, blocks, gate_proj[0], up_proj[0], down_proj[0])
    taken = shifted(send, "c", 1)
    pairs = [(keep[i].astype(F32) + taken[i].astype(F32)).astype(BF) for i in range(4)]
    parts = [pairs[0]] + [shifted(pairs[hop], "x", -hop) for hop in (1, 2, 3)]
    half = after(half, send)
    other_half = shifted(half, "c", 1)
    outgoing_rows = fold(parts, zs, ys)
    student_part, inputs_z = student(
        after(student_order, outgoing_rows), [half, other_half], gathered
    )
    inputs_t = inputs_z.reshape(zs * tokens, input_cols).T
    student_out = lax.psum_scatter(student_part, "z", scatter_dimension=0, tiled=True)
    returned = lax.all_to_all(
        outgoing_rows.reshape(owners, ys * CAP, width // ys),
        fsdp,
        split_axis=0,
        concat_axis=0,
        tiled=True,
    ).reshape(slot_count * ys, width // ys)
    returned, combine = lax.optimization_barrier((returned, combine, inputs_t))[:2]
    teacher = jnp.dot(combine, returned, preferred_element_type=F32).astype(BF)

    teacher = after(teacher, projector_z)
    sums = project(order, gather_expert(teacher), load(after(projector_z, teacher)))
    projected = sums[0]
    for hop in (1, 2, 3):
        projected = projected + shifted(sums[hop], "y", -hop).astype(F32)
    scale = 1.0 / math.sqrt(tokens * owners)
    error = ((student_out.astype(F32) - projected) * scale).astype(BF)

    ahead, behind = [error], [error]
    for hop in (1, 2, 3, 4):
        ahead.append(shifted(ahead[-1], "z", 1))
        if hop < 4:
            behind.append(shifted(behind[-1], "z", -1))
    errors = [error] + ahead[1:] + behind[1:]
    grads = gradient_parts(grad_order, errors, inputs_t)
    gradient = grads[0]
    for hop in (1, 2, 3):
        gradient = gradient + shifted(grads[hop], "y", -hop).astype(F32)
    return (projected.astype(BF), gradient)


def solution(mesh):
    fine = Mesh(mesh.devices.reshape(4, 2, 8, 4), ("x", "c", "z", "y"))
    fsdp, expert = ("z", "y"), ("x", "c")
    return jax.shard_map(
        body,
        mesh=fine,
        in_specs=(
            P(fsdp, None),
            P(fsdp, None),
            P(fsdp, None),
            P(fsdp, None),
            P(fsdp, None, expert),
            P(fsdp, None, expert),
            P(fsdp, expert, None),
            P(fsdp, expert),
            P(fsdp, None),
            P(fsdp, expert),
        ),
        out_specs=(P(fsdp, expert), P(fsdp, expert)),
        check_vma=False,
    )
```

```python
import math

import jax
import jax.numpy as jnp
from jax import lax
from jax.experimental import pallas as pl
from jax.experimental.pallas import tpu as pltpu
from jax.sharding import Mesh
from jax.sharding import PartitionSpec as P

CAP = 4
BF = jnp.bfloat16
F32 = jnp.float32
VMEM = pl.BlockSpec(memory_space=pltpu.VMEM)
SMEM = pl.BlockSpec(memory_space=pltpu.SMEM)


def limit(mib):
    return pltpu.CompilerParams(vmem_limit_bytes=mib * 1024 * 1024)


def after(value, *earlier):
    return lax.optimization_barrier((value, *earlier))[0]


def in_hbm(value):
    return pltpu.with_memory_space_constraint(value, pltpu.HBM)


def shifted(value, axis, hop):
    size = lax.axis_size(axis)
    return lax.ppermute(value, axis, [(i, (i - hop) % size) for i in range(size)])


def gather_expert(value):
    own = [value] + [shifted(value, "x", hop) for hop in (1, 2, 3)]
    other = [shifted(block, "c", 1) for block in own]
    return own + other


def ffn_kernel(order, *refs):
    blocks, hbm, (keep, send), (both, down, near, sems) = refs[:8], refs[8:11], refs[11:13], refs[13:]
    width = blocks[0].shape[1]
    moves = [pltpu.make_async_copy(blocks[k], near.at[k], sems.at[17 + k]) for k in range(4)]
    for move in moves:
        move.start()
    hidden_units = down.shape[0]

    def rows(k):
        return pl.ds(pl.multiple_of(order[k] * width, 128), width)

    copies = [
        pltpu.make_async_copy(
            hbm[i].at[rows(k), :],
            both.at[rows(k), pl.ds(i * hidden_units, hidden_units)],
            sems.at[2 * k + i],
        )
        for k in range(8)
        for i in range(2)
    ] + [pltpu.make_async_copy(hbm[2], down, sems.at[16])]
    for copy in copies:
        copy.start()
    acts = jnp.zeros((blocks[0].shape[0], 2 * hidden_units), F32)
    for k in range(8):
        copies[2 * k].wait()
        copies[2 * k + 1].wait()
        if k < 4:
            moves[k].wait()
        block = near[k] if k < 4 else blocks[k][...]
        acts += jnp.dot(block, both[rows(k), :], preferred_element_type=F32)
    gate_act, up_act = acts[:, :hidden_units], acts[:, hidden_units:]
    copies[16].wait()
    hidden = (gate_act / (1.0 + jnp.exp(-gate_act)) * up_act).astype(BF)
    for k in (4, 5, 6, 7, 0, 1, 2, 3):
        cols = pl.ds(pl.multiple_of(order[k] * width, 128), width)
        part = jnp.dot(hidden, down[:, cols], preferred_element_type=F32).astype(BF)
        if k < 4:
            keep[k] = part
        else:
            send[k - 4] = part


def ffn(order, blocks, gate, up, down):
    rows, width = blocks[0].shape
    shape = jax.ShapeDtypeStruct((4, rows, width), BF)
    return pl.pallas_call(
        ffn_kernel,
        out_shape=(shape, shape),
        in_specs=[SMEM]
        + [pl.BlockSpec(memory_space=pltpu.HBM)] * 4
        + [VMEM] * 4
        + [pl.BlockSpec(memory_space=pltpu.HBM)] * 3,
        out_specs=(VMEM, VMEM),
        scratch_shapes=[pltpu.VMEM((gate.shape[0], 2 * gate.shape[1]), BF), pltpu.VMEM(down.shape, BF)]
        + [pltpu.VMEM((4, rows, width), BF), pltpu.SemaphoreType.DMA((21,))],
        compiler_params=limit(16),
        name="expert_ffn",
    )(order, *map(in_hbm, blocks[:4]), *blocks[4:], in_hbm(gate), in_hbm(up), in_hbm(down))


def fold_kernel(a, b, c, d, out):
    zs, ys, rows, width = out.shape
    total = (a[...].astype(F32) + b[...].astype(F32)) + (c[...].astype(F32) + d[...].astype(F32))
    for y in range(ys):
        part = total[:, y * width : (y + 1) * width]
        out[:, y] = part.reshape(zs, rows, width).astype(BF)


def fold(parts, zs, ys):
    rows, width = parts[0].shape
    return pl.pallas_call(
        fold_kernel,
        out_shape=jax.ShapeDtypeStruct((zs, ys, rows // zs, width // ys), BF),
        in_specs=[VMEM] * 4,
        out_specs=VMEM,
        compiler_params=limit(8),
        name="sum_and_split",
    )(*parts)


def load_kernel(source, target, sem):
    copy = pltpu.make_async_copy(source, target, sem)
    copy.start()
    copy.wait()


def load(value):
    return pl.pallas_call(
        load_kernel,
        out_shape=pltpu.VMEM(value.shape, value.dtype),
        in_specs=[pl.BlockSpec(memory_space=pltpu.HBM)],
        out_specs=VMEM,
        scratch_shapes=[pltpu.SemaphoreType.DMA],
        compiler_params=limit(4),
        name="load",
    )(in_hbm(value))


def project_kernel(order, *refs):
    blocks, projector, outs = refs[:8], refs[8], refs[9:]
    total = jnp.zeros((blocks[0].shape[0], projector.shape[2]), F32)
    for k in range(8):
        total += jnp.dot(blocks[k][...], projector[order[k]], preferred_element_type=F32)
    rows = outs[0].shape[0]
    for i, out in enumerate(outs):
        out[...] = total[i * rows : (i + 1) * rows].astype(out.dtype)


def project(order, blocks, projector):
    tokens, cols = blocks[0].shape[0] // 4, projector.shape[2]
    return pl.pallas_call(
        project_kernel,
        out_shape=[jax.ShapeDtypeStruct((tokens, cols), F32)]
        + [jax.ShapeDtypeStruct((tokens, cols), BF)] * 3,
        in_specs=[SMEM] + [VMEM] * 9,
        out_specs=[VMEM] * 4,
        compiler_params=limit(12),
        name="project",
    )(order, *blocks, projector)


def gradient_kernel(order, *refs):
    blocks, inputs_t, outs, errors, total = refs[:8], refs[8], refs[9:13], refs[13], refs[14]
    tokens = blocks[0].shape[0]
    for k in range(8):
        errors[pl.ds(pl.multiple_of(order[k] * tokens, 128), tokens), :] = blocks[k][...]
    total[...] = jnp.dot(inputs_t[...], errors[...], preferred_element_type=F32)
    rows = outs[0].shape[0]
    for i, out in enumerate(outs):
        out[...] = total[pl.ds(pl.multiple_of(order[8 + i] * rows, 32), rows), :].astype(out.dtype)


def gradient_parts(order, blocks, inputs_t):
    tokens, cols = blocks[0].shape
    rows = inputs_t.shape[0]
    return pl.pallas_call(
        gradient_kernel,
        out_shape=[jax.ShapeDtypeStruct((rows // 4, cols), F32)]
        + [jax.ShapeDtypeStruct((rows // 4, cols), BF)] * 3,
        in_specs=[SMEM] + [VMEM] * 9,
        out_specs=[VMEM] * 4,
        scratch_shapes=[pltpu.VMEM((8 * tokens, cols), BF), pltpu.VMEM((rows, cols), F32)],
        compiler_params=limit(16),
        name="gradient",
    )(order, *blocks, inputs_t)


def student_kernel(order, *refs):
    halves, gathered, outs, (part, inputs, weight, sems) = refs[:2], refs[2], refs[3:5], refs[5:]
    tokens = halves[0].shape[1]
    for k in range(2):
        inputs[:, pl.ds(pl.multiple_of(order[k] * tokens, 32), tokens), :] = halves[k][...]
    keep_inputs = pltpu.make_async_copy(inputs, outs[1], sems.at[0])
    keep_inputs.start()
    rows = weight.shape[0] // 4
    for k in range(4):
        weight[k * rows : (k + 1) * rows, :] = gathered[k, :rows, :]
    flat = inputs[...].reshape(part.shape[0], weight.shape[0])
    part[...] = jnp.dot(flat, weight[...], preferred_element_type=F32).astype(BF)
    keep_part = pltpu.make_async_copy(part, outs[0], sems.at[1])
    keep_part.start()
    keep_inputs.wait()
    keep_part.wait()


def student(order, halves, gathered):
    zs, tokens, width = halves[0].shape
    cols = gathered.shape[2]
    shapes = ((zs * 2 * tokens, cols), (zs, 2 * tokens, width))
    return pl.pallas_call(
        student_kernel,
        out_shape=tuple(pltpu.HBM(shape, BF) for shape in shapes),
        in_specs=[SMEM] + [VMEM] * 3,
        out_specs=(pl.BlockSpec(memory_space=pltpu.HBM),) * 2,
        scratch_shapes=[pltpu.VMEM(shape, BF) for shape in shapes]
        + [pltpu.VMEM((width, cols), BF), pltpu.SemaphoreType.DMA((2,))],
        compiler_params=limit(16),
        name="student",
    )(order, *halves, gathered)


def body(
    teacher_tokens,
    routes,
    slots,
    route_weights,
    gate_proj,
    up_proj,
    down_proj,
    projector,
    student_input,
    student_weight,
):
    fsdp = ("z", "y")
    zs, ys = lax.axis_size("z"), lax.axis_size("y")
    x, c, z, y = (lax.axis_index(name) for name in ("x", "c", "z", "y"))
    owners = zs * ys
    tokens, model = teacher_tokens.shape
    width = model // 8
    slot_count = owners * CAP
    chips = (x + jnp.arange(4, dtype=jnp.int32)) % 4
    order = jnp.concatenate([chips * 2 + c, chips * 2 + (1 - c)])

    weight_rows = student_weight.shape[0]
    in_wave = (routes < owners).T
    info = jnp.concatenate(
        [jnp.where(in_wave, routes.T, -64), jnp.where(in_wave, slots.T, 0), route_weights.T]
    ).astype(BF)
    info = jnp.pad(info, ((0, 24), (0, student_weight.shape[1] - tokens)))
    weight_info = jnp.concatenate([student_weight, info])
    gathered = lax.all_gather(weight_info, "y", axis=0)

    slot_index = jnp.where(routes < owners, routes * CAP + slots, -1).T
    slot_ids = jnp.arange(slot_count, dtype=jnp.int32)[:, None]
    mask = jnp.zeros((slot_count, tokens), F32)
    for k in range(slot_index.shape[0]):
        mask = mask + (slot_index[k][None, :] == slot_ids).astype(F32)
    my_cols = lax.dynamic_slice_in_dim(teacher_tokens, (x * 2 + c) * width, width, 1)
    outgoing = jnp.dot(mask.astype(BF), my_cols, preferred_element_type=F32).astype(BF)
    outgoing = after(outgoing, weight_info)
    arrived = lax.all_to_all(
        outgoing.reshape(owners, CAP, width), fsdp, split_axis=0, concat_axis=0, tiled=True
    ).reshape(slot_count, width)

    projector_z = lax.all_gather(after(projector, weight_info), "z", axis=0, tiled=True).reshape(
        zs, projector.shape[0], projector.shape[1]
    )
    plans = gathered[:, weight_rows : weight_rows + 24, :tokens].astype(F32)
    plans = lax.dynamic_slice_in_dim(jnp.concatenate([plans, plans]), y, ys, 0)
    combine_rows = []
    row_ids = jnp.arange(slot_count * ys, dtype=jnp.int32)[None, :]
    for hop in range(ys):
        plan = plans[hop]
        place = plan[:8] * (ys * CAP) + plan[8:16] + (((y + hop) % ys) * CAP).astype(F32)
        place, share = place.astype(jnp.int32), plan[16:24]
        part = jnp.zeros((tokens, slot_count * ys), F32)
        for k in range(8):
            part = part + jnp.where(place[k][:, None] == row_ids, share[k][:, None], 0.0)
        combine_rows.append(part)
    combine = jnp.concatenate(combine_rows)
    combine = combine.astype(BF)

    eight, four = jnp.arange(8, dtype=jnp.int32), jnp.arange(4, dtype=jnp.int32)
    spots = jnp.where(eight < 5, eight, 4 - eight)
    grad_order = jnp.concatenate([(z + spots) % zs, (y + four) % ys])
    student_order = jnp.concatenate([jnp.stack([c, 1 - c]).astype(jnp.int32)])
    tokens_half = tokens // 2
    input_cols = student_input.shape[1] // zs
    half = lax.dynamic_slice_in_dim(student_input, c * tokens_half, tokens_half, 0)
    half = half.reshape(tokens_half, zs, input_cols).transpose(1, 0, 2)
    arrived, order, grad_order, student_order, half = lax.optimization_barrier(
        (arrived, order, grad_order, student_order, half)
    )
    half = lax.all_to_all(half, "z", split_axis=0, concat_axis=0, tiled=True)

    blocks = gather_expert(arrived)
    keep, send = ffn(order, blocks, gate_proj[0], up_proj[0], down_proj[0])
    taken = shifted(send, "c", 1)
    pairs = [(keep[i].astype(F32) + taken[i].astype(F32)).astype(BF) for i in range(4)]
    parts = [pairs[0]] + [shifted(pairs[hop], "x", -hop) for hop in (1, 2, 3)]
    half = after(half, send)
    other_half = shifted(half, "c", 1)
    outgoing_rows = fold(parts, zs, ys)
    student_part, inputs_z = student(
        after(student_order, outgoing_rows), [half, other_half], gathered
    )
    inputs_t = inputs_z.reshape(zs * tokens, input_cols).T
    student_out = lax.psum_scatter(student_part, "z", scatter_dimension=0, tiled=True)
    returned = lax.all_to_all(
        outgoing_rows.reshape(owners, ys * CAP, width // ys),
        fsdp,
        split_axis=0,
        concat_axis=0,
        tiled=True,
    ).reshape(slot_count * ys, width // ys)
    returned, combine = lax.optimization_barrier((returned, combine, inputs_t))[:2]
    teacher = jnp.dot(combine, returned, preferred_element_type=F32).astype(BF)

    teacher = after(teacher, projector_z)
    sums = project(order, gather_expert(teacher), load(after(projector_z, teacher)))
    projected = sums[0]
    for hop in (1, 2, 3):
        projected = projected + shifted(sums[hop], "y", -hop).astype(F32)
    scale = 1.0 / math.sqrt(tokens * owners)
    error = ((student_out.astype(F32) - projected) * scale).astype(BF)

    ahead, behind = [error], [error]
    for hop in (1, 2, 3, 4):
        ahead.append(shifted(ahead[-1], "z", 1))
        if hop < 4:
            behind.append(shifted(behind[-1], "z", -1))
    errors = [error] + ahead[1:] + behind[1:]
    grads = gradient_parts(grad_order, errors, inputs_t)
    gradient = grads[0]
    for hop in (1, 2, 3):
        gradient = gradient + shifted(grads[hop], "y", -hop).astype(F32)
    return (projected.astype(BF), gradient)


def solution(mesh):
    fine = Mesh(mesh.devices.reshape(4, 2, 8, 4), ("x", "c", "z", "y"))
    fsdp, expert = ("z", "y"), ("x", "c")
    return jax.shard_map(
        body,
        mesh=fine,
        in_specs=(
            P(fsdp, None),
            P(fsdp, None),
            P(fsdp, None),
            P(fsdp, None),
            P(fsdp, None, expert),
            P(fsdp, None, expert),
            P(fsdp, expert, None),
            P(fsdp, expert),
            P(fsdp, None),
            P(fsdp, expert),
        ),
        out_specs=(P(fsdp, expert), P(fsdp, expert)),
        check_vma=False,
    )
```
